256 devices in a mesh: row: 16 (over z_hi, y, core), col: 16 (over x, z_lo).
Axes of the slice: x: 4, y: 4, z: 8 (z_hi: 2, z_lo: 4; z = z_hi * 4 + z_lo), core: 2. Of those that a mesh axis runs over, the one named last changes fastest.
Arguments:
- features: bfloat16 [65536, 256], P(('col', 'row')), may hold values from -6 to 6
- adj_tiles: bfloat16 [16, 16, 80, 256, 256], P('row', 'col'), may hold values from -0.078125 to 0.078125
- tile_rows: int32 [16, 16, 80], P('row', 'col'), may hold values from 0 to 15, as said below
- tile_cols: int32 [16, 16, 80], P('row', 'col'), may hold values from 0 to 15, as said below
- tile_count: int32 [16, 16], P('row', 'col'), may hold values from 1 to 80, as said below
- weight: bfloat16 [256, 256], replicated, may hold values from -0.375 to 0.375
- grad_out: bfloat16 [65536, 256], P(('row', 'col')), may hold values from -6 to 6
Outputs:
- activation: bfloat16 [65536, 256], P(('row', 'col'))
- weight_grad: float32 [256, 256], replicated
- x_grad: bfloat16 [65536, 256], P(('col', 'row'))
The draws below stay inside these ranges and needn't reach their ends.
Inputs may be any that keep to these rules, and one draw needn't show every extreme that they name: On each grid block the 80 slots name distinct tile positions (tile_rows, tile_cols). `tile_cols`: paired with tile_rows slot by slot. `tile_count`: slots of a grid block at or beyond its count are ignored.
All inputs are finite; a program needn't handle non-finite values.
Results may differ from the reference program's by a relative error of at most 0.025.
Values may be sent and summed in bfloat16 or wider, within the bound.
No kernel may reach another device: no remote copies, remote signals or barrier semaphores. Data moves between devices by JAX's collectives and lax.ppermute only.
A program may use at most 128 MiB of HBM per device.

```python
import math
import jax
import jax.numpy as jnp
from jax import lax

F = 256
TILE = 256
ROWS_DEV = 256
NODES = 65536
BR = 16
BC = 16
TILES_DEV = 80
N_ROW = 16
N_COL = 16


def tile_positions(key):
    position_total = BR * BC
    device_total = N_ROW * N_COL
    spots = jnp.arange(position_total, dtype=jnp.int32)

    def rank_one(subkey, device_id):
        scores = jax.random.randint(subkey, (position_total,), 0, 1 << 19) * position_total + spots
        forced = jnp.where(device_id == 0, position_total - 1, 0)
        scores = jnp.where((device_id < 2) & (spots == forced), -1, scores)
        return jnp.argsort(scores, stable=True)[:TILES_DEV].astype(jnp.int32)
    device_keys = jax.random.split(jax.random.fold_in(key, 11), device_total)
    chosen = jax.vmap(rank_one)(device_keys, jnp.arange(device_total, dtype=jnp.int32))
    return chosen.reshape(N_ROW, N_COL, TILES_DEV)


def draw_tile_rows(key, part):
    return tile_positions(key) // BC


def draw_tile_cols(key, part):
    return tile_positions(key) % BC


def draw_tile_count(key, part):
    device_total = N_ROW * N_COL
    subkeys = jax.random.split(jax.random.fold_in(key, 23), 4)
    factor_one = jax.random.randint(subkeys[0], (device_total,), 1, TILES_DEV + 1)
    factor_two = jax.random.randint(subkeys[1], (device_total,), 1, TILES_DEV + 1)
    counts = jnp.maximum(1, factor_one * factor_two // TILES_DEV)
    device_ids = jnp.arange(device_total, dtype=jnp.int32)
    busiest = jax.random.randint(subkeys[2], (), 0, device_total)
    lightest = (busiest + 1 + jax.random.randint(subkeys[3], (), 0, device_total - 1)) % device_total
    counts = jnp.where(device_ids == busiest, TILES_DEV, counts)
    counts = jnp.where(device_ids == lightest, 1, counts)
    return counts.reshape(N_ROW, N_COL).astype(jnp.int32)


def shard_levels(key, dims, pieces, low, largest):
    def one(dim, blocks):
        steps = jax.random.uniform(jax.random.fold_in(jax.random.fold_in(key, 6), dim), (blocks,), jnp.float32, low / len(pieces), largest / len(pieces))
        return jnp.repeat(jnp.exp(steps), dims[dim] // blocks).reshape((-1,) + (1,) * (len(dims) - dim - 1))

    level = one(*pieces[0])
    for cut in pieces[1:]:
        level = level * one(*cut)
    return level


def normal_values(own_key, dims, scale, reach, cuts=(), held_as=jnp.bfloat16):
    drawn = scale * jax.random.normal(own_key, dims, jnp.float32)
    if cuts:
        drawn = drawn * shard_levels(own_key, dims, cuts, -0.22, 0.18)
    return jnp.clip(drawn, -reach, reach).astype(held_as)


def setup_inputs(seed: int = 0) -> dict:
    streams_of = jax.random.split(jax.random.key(seed), 8)
    features = normal_values(streams_of[0], (NODES, F), 1.0, 6.0, ((0, 256),))
    adj_tiles = normal_values(streams_of[1], (N_ROW, N_COL, TILES_DEV, TILE, TILE), (max(1, TILES_DEV * TILE * TILE // (4 * ROWS_DEV))) ** -0.5, 0.078125, ((0, 16), (1, 16)))
    tile_rows = draw_tile_rows(jax.random.fold_in(streams_of[7], 71), 0)
    tile_cols = draw_tile_cols(jax.random.fold_in(streams_of[7], 71), 0)
    tile_count = draw_tile_count(jax.random.fold_in(streams_of[7], 71), 0)
    weight = normal_values(streams_of[5], (F, F), F ** -0.5, 0.375)
    grad_out = normal_values(streams_of[6], (NODES, F), 1.0, 6.0, ((0, 256),))
    return dict(features=features, adj_tiles=adj_tiles, tile_rows=tile_rows, tile_cols=tile_cols, tile_count=tile_count, weight=weight, grad_out=grad_out)


def reference(features, adj_tiles, tile_rows, tile_cols, tile_count, weight, grad_out):
    block_rows = BR * TILE
    block_cols = BC * TILE
    slot_ids = jnp.arange(TILES_DEV, dtype=jnp.int32)

    def forward_block(block_row):

        def over_cols(running, block_col):
            blocks = adj_tiles[block_row, block_col].astype(jnp.float32)
            row_ids = tile_rows[block_row, block_col]
            col_ids = tile_cols[block_row, block_col]
            active = (slot_ids < tile_count[block_row, block_col]).astype(jnp.float32)
            col_panel = lax.dynamic_slice_in_dim(features, (block_col * block_cols).astype(jnp.int32), block_cols, 0)
            col_panel = col_panel.reshape(BC, TILE, F).astype(jnp.float32)
            product = jnp.einsum('gij,gjf->gif', blocks, col_panel[col_ids]) * active[:, None, None]
            partial_sum = jnp.zeros((BR, TILE, F), jnp.float32).at[row_ids].add(product)
            rounded = lax.optimization_barrier(partial_sum.astype(jnp.bfloat16))
            return (running + rounded.astype(jnp.float32), None)
        running, _ = lax.scan(over_cols, jnp.zeros((BR, TILE, F), jnp.float32), jnp.arange(N_COL, dtype=jnp.int32))
        return running.astype(jnp.bfloat16)
    aggregated = lax.map(forward_block, jnp.arange(N_ROW, dtype=jnp.int32)).reshape(NODES, F)
    pre_act = jnp.dot(aggregated, weight, preferred_element_type=jnp.float32)
    gate_sig = jax.nn.sigmoid(pre_act)
    activation = (pre_act * gate_sig).astype(jnp.bfloat16)
    silu_slope = gate_sig * (1.0 + pre_act * (1.0 - gate_sig))
    act_grad = (grad_out.astype(jnp.float32) * silu_slope).astype(jnp.bfloat16)
    grad_scale = 1.0 / math.sqrt(NODES)
    weight_grad = lax.dot_general(aggregated, act_grad, (((0,), (0,)), ((), ())), preferred_element_type=jnp.float32) * grad_scale
    msg_grad = jnp.dot(act_grad, weight.T, preferred_element_type=jnp.float32).astype(jnp.bfloat16)

    def backward_block(block_col):

        def over_rows(running, block_row):
            blocks = adj_tiles[block_row, block_col].astype(jnp.float32)
            row_ids = tile_rows[block_row, block_col]
            col_ids = tile_cols[block_row, block_col]
            active = (slot_ids < tile_count[block_row, block_col]).astype(jnp.float32)
            row_panel = lax.dynamic_slice_in_dim(msg_grad, (block_row * block_rows).astype(jnp.int32), block_rows, 0)
            row_panel = row_panel.reshape(BR, TILE, F).astype(jnp.float32)
            product = jnp.einsum('gij,gif->gjf', blocks, row_panel[row_ids]) * active[:, None, None]
            partial_sum = jnp.zeros((BC, TILE, F), jnp.float32).at[col_ids].add(product)
            rounded = lax.optimization_barrier(partial_sum.astype(jnp.bfloat16))
            return (running + rounded.astype(jnp.float32), None)
        running, _ = lax.scan(over_rows, jnp.zeros((BC, TILE, F), jnp.float32), jnp.arange(N_ROW, dtype=jnp.int32))
        return running.astype(jnp.bfloat16)
    x_grad = lax.map(backward_block, jnp.arange(N_COL, dtype=jnp.int32)).reshape(NODES, F)
    return (activation, weight_grad, x_grad)
```

```python
import functools
import math

import jax
import jax.numpy as jnp
from jax import lax
from jax.experimental import pallas as pl
from jax.experimental.pallas import tpu as pltpu
from jax.sharding import PartitionSpec as P

ROW_DEVICES = 16
COL_DEVICES = 16
UNROLL = 4
VMEM_BYTES = 60 << 20
BF16 = jnp.bfloat16
F32 = jnp.float32


def row_permute(value, zh=0, y=0, core=0):
    pairs = []
    for i in range(ROW_DEVICES):
        to_zh, to_y, to_core = (i >> 3) ^ zh, (((i >> 1) & 3) + y) % 4, (i & 1) ^ core
        pairs.append((i, (to_zh * 4 + to_y) * 2 + to_core))
    return lax.ppermute(value, "row", pairs)


def col_permute(value, x=0, zl=0):
    pairs = []
    for i in range(COL_DEVICES):
        pairs.append((i, (((i >> 2) + x) % 4) * 4 + ((i & 3) + zl) % 4))
    return lax.ppermute(value, "col", pairs)


def row_tile(k, j, flip):
    index = lax.axis_index("row")
    zh, y, core = index >> 3, (index >> 1) & 3, index & 1
    return ((zh ^ j) * 4 + ((y + k) & 3)) * 2 + (core ^ flip)


def col_tile(k, j):
    index = lax.axis_index("col")
    return (((index >> 2) + k) & 3) * 4 + ((index + j) & 3)


def tile_loop(count, into, frm, tiles, panel, tile_buf, acc, tile_sem, piece_copies, contract):
    @pl.loop(0, count)
    def _(i):
        pltpu.make_async_copy(tiles.at[i], tile_buf.at[i], tile_sem.at[i]).start()

    for copy in piece_copies:
        copy.start()

    @pl.loop(0, acc.shape[0])
    def _(i):
        acc[i] = jnp.zeros(acc.shape[1:], F32)

    for copy in piece_copies:
        copy.wait()

    def arrive(i):
        pltpu.make_async_copy(tiles.at[i], tile_buf.at[i], tile_sem.at[i]).wait()

    def product(i):
        return lax.dot_general(
            tile_buf[i], panel[frm[i]], (((contract,), (0,)), ((), ())), preferred_element_type=F32
        )

    groups = count // UNROLL

    @pl.loop(0, groups)
    def _(group):
        first = group * UNROLL
        for j in range(UNROLL):
            arrive(first + j)
        terms = [product(first + j) for j in range(UNROLL)]
        for j in range(UNROLL):
            acc[into[first + j]] += terms[j]

    @pl.loop(groups * UNROLL, count)
    def _(i):
        arrive(i)
        acc[into[i]] += product(i)


def forward_kernel(cnt, into, frm, near, far, tiles, o0, o1, o2, o3, panel, tile_buf, acc, tile_sem, piece_sem):
    copies = []
    for flip, piece in enumerate((near, far)):
        for k in range(4):
            for j in range(2):
                n = k * 2 + j
                copies.append(
                    pltpu.make_async_copy(
                        piece.at[n], panel.at[row_tile(-k, j, flip)], piece_sem.at[flip * 8 + n]
                    )
                )
    tile_loop(cnt[0], into, frm, tiles, panel, tile_buf, acc, tile_sem, copies, 1)
    for k, out in enumerate((o0, o1, o2, o3)):
        for j in range(4):
            out[j] = acc[col_tile(k, j)].astype(BF16)


def backward_kernel(cnt, into, frm, g0, g1, g2, g3, tiles, own, sent, panel, tile_buf, acc, tile_sem, piece_sem):
    copies = []
    for k, piece in enumerate((g0, g1, g2, g3)):
        for j in range(4):
            copies.append(
                pltpu.make_async_copy(
                    piece.at[j], panel.at[col_tile(-k, -j)], piece_sem.at[k * 4 + j]
                )
            )
    tile_loop(cnt[0], into, frm, tiles, panel, tile_buf, acc, tile_sem, copies, 0)
    for flip, out in enumerate((own, sent)):
        for k in range(4):
            for j in range(2):
                out[k * 2 + j] = acc[row_tile(k, j, flip)].astype(BF16)


def tile_call(kernel, name, cnt, into, frm, pieces, tiles, out_shapes):
    slots, edge, _ = tiles.shape
    smem = pl.BlockSpec(memory_space=pltpu.SMEM)
    hbm = pl.BlockSpec(memory_space=pl.ANY)
    return pl.pallas_call(
        kernel,
        out_shape=[jax.ShapeDtypeStruct(shape, BF16) for shape in out_shapes],
        in_specs=[smem] * 3 + [hbm] * (len(pieces) + 1),
        out_specs=[pl.BlockSpec(memory_space=pltpu.VMEM)] * len(out_shapes),
        scratch_shapes=[
            pltpu.VMEM((16, edge, edge), BF16),
            pltpu.VMEM((slots, edge, edge), BF16),
            pltpu.VMEM((16, edge, edge), F32),
            pltpu.SemaphoreType.DMA((slots,)),
            pltpu.SemaphoreType.DMA((16,)),
        ],
        compiler_params=pltpu.CompilerParams(vmem_limit_bytes=VMEM_BYTES),
        cost_estimate=pl.CostEstimate(
            flops=2 * slots * edge**3, bytes_accessed=slots * edge * edge * 2, transcendentals=0
        ),
        name=name,
    )(cnt, into, frm, *pieces, tiles)


def dense_kernel(own, q1, q2, q3, weight, grad_out, activation, msg_grad, weight_term):
    total = own[...] + q1[...].astype(F32) + q2[...].astype(F32) + q3[...].astype(F32)
    aggregated = total.astype(BF16)
    pre_act = jnp.dot(aggregated, weight[...], preferred_element_type=F32)
    gate_sig = 1.0 / (1.0 + jnp.exp(-pre_act))
    activation[...] = (pre_act * gate_sig).astype(BF16)
    slope = gate_sig * (1.0 + pre_act * (1.0 - gate_sig))
    act_grad = (grad_out[...].astype(F32) * slope).astype(BF16)
    weight_term[...] = lax.dot_general(
        aggregated, act_grad, (((0,), (0,)), ((), ())), preferred_element_type=F32
    )
    msg_grad[...] = lax.dot_general(
        act_grad, weight[...], (((1,), (1,)), ((), ())), preferred_element_type=F32
    ).astype(BF16)


def dense_call(own, q1, q2, q3, weight, grad_out):
    shape = grad_out.shape
    return pl.pallas_call(
        dense_kernel,
        out_shape=[
            jax.ShapeDtypeStruct(shape, BF16),
            jax.ShapeDtypeStruct(shape, BF16),
            jax.ShapeDtypeStruct(weight.shape, F32),
        ],
        cost_estimate=pl.CostEstimate(flops=6 * 256**3, bytes_accessed=10**6, transcendentals=65536),
        name="dense",
    )(own, q1, q2, q3, weight, grad_out)


def ordered_sum(pieces, position):
    stacked = jnp.stack(pieces)
    total = lax.dynamic_index_in_dim(stacked, position & 3, 0, keepdims=False)
    for place in range(1, 4):
        total = total + lax.dynamic_index_in_dim(stacked, (position - place) & 3, 0, keepdims=False)
    return total


def reduce_weight(term):
    row, col = lax.axis_index("row"), lax.axis_index("col")
    zh, y, core = row >> 3, (row >> 1) & 3, row & 1
    x, zl = col >> 2, col & 3
    width = term.shape[1]

    def part(value, index, count):
        rows = value.shape[0] // count
        return lax.dynamic_slice_in_dim(value, index * rows, rows, 0)

    half = part(term, core, 2) + row_permute(part(term, core ^ 1, 2), core=1)
    eighth = part(half, y, 4)
    for k in range(1, 4):
        eighth = eighth + row_permute(part(half, (y + k) & 3, 4), y=k)
    mine = part(eighth, zh, 2) + row_permute(part(eighth, zh ^ 1, 2), zh=1)
    mine = ordered_sum([mine] + [col_permute(mine, x=k) for k in (1, 2, 3)], x)
    mine = ordered_sum([mine] + [col_permute(mine, zl=k) for k in (1, 2, 3)], zl)
    other = row_permute(mine, zh=1)
    pair = jnp.where(zh == 0, jnp.stack([mine, other]), jnp.stack([other, mine]))
    pair = pair.reshape(-1, width)
    quads = jnp.stack([pair] + [row_permute(pair, y=k) for k in (1, 2, 3)])
    quads = jnp.stack(
        [lax.dynamic_index_in_dim(quads, (y - place) & 3, 0, keepdims=False) for place in range(4)]
    ).reshape(-1, width)
    sibling = row_permute(quads, core=1)
    whole = jnp.where(core == 0, jnp.stack([quads, sibling]), jnp.stack([sibling, quads]))
    return whole.reshape(-1, width)


def add_all(pieces):
    total = pieces[0].astype(F32)
    for piece in pieces[1:]:
        total = total + piece.astype(F32)
    return total


def local(features, adj_tiles, tile_rows, tile_cols, tile_count, weight, grad_out):
    tiles = adj_tiles[0, 0]
    row_ids, col_ids, count = tile_rows[0, 0], tile_cols[0, 0], tile_count[0]
    edge, width = features.shape
    node_total = edge * ROW_DEVICES * COL_DEVICES

    with jax.named_scope("gather_features"):
        pair = jnp.stack([features, row_permute(features, zh=1)])
        near = jnp.concatenate([pair] + [row_permute(pair, y=k) for k in (1, 2, 3)])
        far = row_permute(near, core=1)

    parts = tile_call(
        forward_kernel, "forward_tiles", count, row_ids, col_ids, [near, far], tiles, [(4, edge, width)] * 4
    )

    with jax.named_scope("reduce_aggregate"):
        parts = [parts[0]] + [col_permute(parts[k], x=k) for k in (1, 2, 3)]
        sums = [add_all([part[j] for part in parts]) for j in range(4)]
        arrived = [col_permute(sums[k].astype(BF16), zl=k) for k in (1, 2, 3)]

    activation, msg_grad, weight_term = dense_call(sums[0], *arrived, weight, grad_out)

    with jax.named_scope("gather_messages"):
        group = jnp.stack([msg_grad] + [col_permute(msg_grad, zl=k) for k in (1, 2, 3)])
        groups = [group] + [col_permute(group, x=k) for k in (1, 2, 3)]

    with jax.named_scope("reduce_weight"):
        weight_grad = reduce_weight(weight_term) * (1.0 / math.sqrt(node_total))

    own, sent = tile_call(
        backward_kernel, "backward_tiles", count, col_ids, row_ids, groups, tiles, [(8, edge, width)] * 2
    )

    with jax.named_scope("reduce_features"):
        both = add_all([own, row_permute(sent, core=1)]).astype(BF16).reshape(4, 2, edge, width)
        quads = [both[0]] + [row_permute(both[k], y=k) for k in (1, 2, 3)]
        kept = add_all([quad[0] for quad in quads])
        given = add_all([quad[1] for quad in quads]).astype(BF16)
        x_grad = (kept + row_permute(given, zh=1).astype(F32)).astype(BF16)

    return (activation, weight_grad, x_grad)


def solution(mesh):
    return jax.shard_map(
        local,
        mesh=mesh,
        in_specs=(
            P(("col", "row"), None),
            P("row", "col", None, None, None),
            P("row", "col", None),
            P("row", "col", None),
            P("row", "col"),
            P(),
            P(("row", "col"), None),
        ),
        out_specs=(P(("row", "col"), None), P(), P(("col", "row"), None)),
        check_vma=False,
    )
```

```python
import functools
import math

import jax
import jax.numpy as jnp
from jax import lax
from jax.experimental import pallas as pl
from jax.experimental.pallas import tpu as pltpu
from jax.sharding import PartitionSpec as P

ROW_DEVICES = 16
COL_DEVICES = 16
UNROLL = 4
FORWARD_PARTS = 2
BACKWARD_PARTS = 1
VMEM_BYTES = 48 << 20
BF16 = jnp.bfloat16
F32 = jnp.float32


def row_permute(value, zh=0, y=0, core=0):
    pairs = []
    for i in range(ROW_DEVICES):
        to_zh, to_y, to_core = (i >> 3) ^ zh, (((i >> 1) & 3) + y) % 4, (i & 1) ^ core
        pairs.append((i, (to_zh * 4 + to_y) * 2 + to_core))
    return lax.ppermute(value, "row", pairs)


def col_permute(value, x=0, zl=0):
    pairs = []
    for i in range(COL_DEVICES):
        pairs.append((i, (((i >> 2) + x) % 4) * 4 + ((i & 3) + zl) % 4))
    return lax.ppermute(value, "col", pairs)


def row_tile(k, j, flip):
    index = lax.axis_index("row")
    zh, y, core = index >> 3, (index >> 1) & 3, index & 1
    return ((zh ^ j) * 4 + ((y + k) & 3)) * 2 + (core ^ flip)


def col_tile(k, j):
    index = lax.axis_index("col")
    return (((index >> 2) + k) & 3) * 4 + ((index + j) & 3)


def tile_loop(count, into, frm, tiles, panel, tile_buf, acc, tile_sem, piece_copies, contract):
    @pl.loop(0, count)
    def _(i):
        pltpu.make_async_copy(tiles.at[i], tile_buf.at[i], tile_sem.at[i]).start()

    for copy in piece_copies:
        copy.start()

    @pl.loop(0, acc.shape[0])
    def _(i):
        acc[i] = jnp.zeros(acc.shape[1:], F32)

    for copy in piece_copies:
        copy.wait()

    def arrive(i):
        pltpu.make_async_copy(tiles.at[i], tile_buf.at[i], tile_sem.at[i]).wait()

    def product(i):
        return lax.dot_general(
            tile_buf[i], panel[frm[i]], (((contract,), (0,)), ((), ())), preferred_element_type=F32
        )

    groups = count // UNROLL

    @pl.loop(0, groups)
    def _(group):
        first = group * UNROLL
        for j in range(UNROLL):
            arrive(first + j)
        terms = [product(first + j) for j in range(UNROLL)]
        for j in range(UNROLL):
            acc[into[first + j]] += terms[j]

    @pl.loop(groups * UNROLL, count)
    def _(i):
        arrive(i)
        acc[into[i]] += product(i)


def forward_kernel(cnt, into, frm, near, far, tiles, o0, o1, o2, o3, panel, tile_buf, acc, tile_sem, piece_sem):
    copies = []
    for flip, piece in enumerate((near, far)):
        for k in range(4):
            for j in range(2):
                n = k * 2 + j
                copies.append(
                    pltpu.make_async_copy(
                        piece.at[n], panel.at[row_tile(-k, j, flip)], piece_sem.at[flip * 8 + n]
                    )
                )
    tile_loop(cnt[0], into, frm, tiles, panel, tile_buf, acc, tile_sem, copies, 1)
    for k, out in enumerate((o0, o1, o2, o3)):
        for j in range(4):
            out[j] = acc[col_tile(k, j)].astype(BF16)


def backward_kernel(cnt, into, frm, g0, g1, g2, g3, tiles, own, sent, panel, tile_buf, acc, tile_sem, piece_sem):
    copies = []
    for k, piece in enumerate((g0, g1, g2, g3)):
        for j in range(4):
            copies.append(
                pltpu.make_async_copy(
                    piece.at[j], panel.at[col_tile(-k, -j)], piece_sem.at[k * 4 + j]
                )
            )
    tile_loop(cnt[0], into, frm, tiles, panel, tile_buf, acc, tile_sem, copies, 0)
    for flip, out in enumerate((own, sent)):
        for k in range(4):
            for j in range(2):
                out[k * 2 + j] = acc[row_tile(k, j, flip)].astype(BF16)


def tile_call(kernel, name, cnt, into, frm, pieces, tiles, out_shapes):
    slots, edge, _ = tiles.shape
    width = pieces[0].shape[-1]
    smem = pl.BlockSpec(memory_space=pltpu.SMEM)
    hbm = pl.BlockSpec(memory_space=pl.ANY)
    return pl.pallas_call(
        kernel,
        out_shape=[jax.ShapeDtypeStruct(shape, BF16) for shape in out_shapes],
        in_specs=[smem] * 3 + [hbm] * (len(pieces) + 1),
        out_specs=[pl.BlockSpec(memory_space=pltpu.VMEM)] * len(out_shapes),
        scratch_shapes=[
            pltpu.VMEM((16, edge, width), BF16),
            pltpu.VMEM((slots, edge, edge), BF16),
            pltpu.VMEM((16, edge, width), F32),
            pltpu.SemaphoreType.DMA((slots,)),
            pltpu.SemaphoreType.DMA((16,)),
        ],
        compiler_params=pltpu.CompilerParams(vmem_limit_bytes=VMEM_BYTES),
        cost_estimate=pl.CostEstimate(
            flops=2 * slots * edge**3, bytes_accessed=slots * edge * edge * 2, transcendentals=0
        ),
        name=name,
    )(cnt, into, frm, *pieces, tiles)


def dense_kernel(*refs):
    aggregated = []
    for part in range(FORWARD_PARTS):
        own, q1, q2, q3 = refs[4 * part : 4 * part + 4]
        total = own[...] + q1[...].astype(F32) + q2[...].astype(F32) + q3[...].astype(F32)
        aggregated.append(total.astype(BF16))
    weight, grad_out, activation, weight_term = refs[4 * FORWARD_PARTS : 4 * FORWARD_PARTS + 4]
    msg_parts = refs[4 * FORWARD_PARTS + 4 :]
    step = weight.shape[0] // FORWARD_PARTS
    pre_act = jnp.zeros(grad_out.shape, F32)
    for part in range(FORWARD_PARTS):
        pre_act += jnp.dot(
            aggregated[part], weight[part * step : (part + 1) * step], preferred_element_type=F32
        )
    gate_sig = 1.0 / (1.0 + jnp.exp(-pre_act))
    activation[...] = (pre_act * gate_sig).astype(BF16)
    slope = gate_sig * (1.0 + pre_act * (1.0 - gate_sig))
    act_grad = (grad_out[...].astype(F32) * slope).astype(BF16)
    for part in range(FORWARD_PARTS):
        weight_term[part * step : (part + 1) * step] = lax.dot_general(
            aggregated[part], act_grad, (((0,), (0,)), ((), ())), preferred_element_type=F32
        )
    msg_grad = lax.dot_general(
        act_grad, weight[...], (((1,), (1,)), ((), ())), preferred_element_type=F32
    ).astype(BF16)
    step = weight.shape[0] // BACKWARD_PARTS
    for part in range(BACKWARD_PARTS):
        msg_parts[part][...] = msg_grad[:, part * step : (part + 1) * step]


def dense_call(sums, weight, grad_out):
    rows, width = grad_out.shape
    return pl.pallas_call(
        dense_kernel,
        out_shape=[
            jax.ShapeDtypeStruct(grad_out.shape, BF16),
            jax.ShapeDtypeStruct(weight.shape, F32),
        ]
        + [jax.ShapeDtypeStruct((rows, width // BACKWARD_PARTS), BF16)] * BACKWARD_PARTS,
        compiler_params=pltpu.CompilerParams(vmem_limit_bytes=8 << 20),
        cost_estimate=pl.CostEstimate(flops=6 * 256**3, bytes_accessed=10**6, transcendentals=65536),
        name="dense",
    )(*sums, weight, grad_out)


def ordered_sum(pieces, position):
    stacked = jnp.stack(pieces)
    total = lax.dynamic_index_in_dim(stacked, position & 3, 0, keepdims=False)
    for place in range(1, 4):
        total = total + lax.dynamic_index_in_dim(stacked, (position - place) & 3, 0, keepdims=False)
    return total


def part_of(value, index, count):
    rows = value.shape[0] // count
    return lax.dynamic_slice_in_dim(value, index * rows, rows, 0)


def scatter_weight(term):
    row = lax.axis_index("row")
    zh, y, core = row >> 3, (row >> 1) & 3, row & 1
    half = part_of(term, core, 2) + row_permute(part_of(term, core ^ 1, 2), core=1)
    eighth = part_of(half, y, 4)
    for k in range(1, 4):
        eighth = eighth + row_permute(part_of(half, (y + k) & 3, 4), y=k)
    return part_of(eighth, zh, 2) + row_permute(part_of(eighth, zh ^ 1, 2), zh=1)


def add_over_x(mine):
    x = lax.axis_index("col") >> 2
    return ordered_sum([mine] + [col_permute(mine, x=k) for k in (1, 2, 3)], x)


def add_over_zl(mine):
    zl = lax.axis_index("col") & 3
    return ordered_sum([mine] + [col_permute(mine, zl=k) for k in (1, 2, 3)], zl)


def gather_zh(mine):
    other = row_permute(mine, zh=1)
    low = (lax.axis_index("row") >> 3) == 0
    pair = jnp.where(low, jnp.stack([mine, other]), jnp.stack([other, mine]))
    return pair.reshape(-1, mine.shape[1])


def gather_y_core(pair):
    row = lax.axis_index("row")
    y, core = (row >> 1) & 3, row & 1
    width = pair.shape[1]
    quads = jnp.stack([pair] + [row_permute(pair, y=k) for k in (1, 2, 3)])
    quads = jnp.stack(
        [lax.dynamic_index_in_dim(quads, (y - place) & 3, 0, keepdims=False) for place in range(4)]
    ).reshape(-1, width)
    sibling = row_permute(quads, core=1)
    whole = jnp.where(core == 0, jnp.stack([quads, sibling]), jnp.stack([sibling, quads]))
    return whole.reshape(-1, width)


def add_all(pieces):
    total = pieces[0].astype(F32)
    for piece in pieces[1:]:
        total = total + piece.astype(F32)
    return total


def split_columns(value, parts):
    step = value.shape[-1] // parts
    return [value[..., part * step : (part + 1) * step] for part in range(parts)]


def forward_part(features, count, row_ids, col_ids, tiles):
    edge, width = features.shape
    with jax.named_scope("gather_features"):
        pair = jnp.stack([features, row_permute(features, zh=1)])
        near = jnp.concatenate([pair] + [row_permute(pair, y=k) for k in (1, 2, 3)])
        far = row_permute(near, core=1)
    parts = tile_call(
        forward_kernel, "forward_tiles", count, row_ids, col_ids, [near, far], tiles, [(4, edge, width)] * 4
    )
    with jax.named_scope("reduce_aggregate"):
        parts = [parts[0]] + [col_permute(parts[k], x=k) for k in (1, 2, 3)]
        sums = [add_all([part[j] for part in parts]) for j in range(4)]
        return [sums[0]] + [col_permute(sums[k].astype(BF16), zl=k) for k in (1, 2, 3)]


def gather_messages(msg_grad):
    with jax.named_scope("gather_messages"):
        group = jnp.stack([msg_grad] + [col_permute(msg_grad, zl=k) for k in (1, 2, 3)])
        return [group] + [col_permute(group, x=k) for k in (1, 2, 3)]


def local(features, adj_tiles, tile_rows, tile_cols, tile_count, weight, grad_out):
    tiles = adj_tiles[0, 0]
    row_ids, col_ids, count = tile_rows[0, 0], tile_cols[0, 0], tile_count[0]
    edge = features.shape[0]
    node_total = edge * ROW_DEVICES * COL_DEVICES

    sums = []
    for piece in split_columns(features, FORWARD_PARTS):
        sums += forward_part(piece, count, row_ids, col_ids, tiles)

    activation, weight_term, *msg_parts = dense_call(sums, weight, grad_out)

    groups = [gather_messages(piece) for piece in msg_parts]
    with jax.named_scope("scatter_weight"):
        mine = add_over_zl(scatter_weight(weight_term))
        mine, groups[-1] = lax.optimization_barrier((mine, groups[-1]))
        mine = add_over_x(mine)

    x_grads = []
    for part, group in enumerate(groups):
        width = group[0].shape[-1]
        own, sent = tile_call(
            backward_kernel, "backward_tiles", count, col_ids, row_ids, group, tiles, [(8, edge, width)] * 2
        )
        last = part == BACKWARD_PARTS - 1
        if last:
            mine, own, sent = lax.optimization_barrier((mine, own, sent))
        with jax.named_scope("reduce_features"):
            both = add_all([own, row_permute(sent, core=1)]).astype(BF16).reshape(4, 2, edge, width)
            if last:
                both, mine = lax.optimization_barrier((both, mine))
            quads = [both[0]] + [row_permute(both[k], y=k) for k in (1, 2, 3)]
            kept = add_all([quad[0] for quad in quads])
            given = add_all([quad[1] for quad in quads]).astype(BF16)
            if last:
                with jax.named_scope("gather_weight"):
                    mine = gather_zh(mine)
                    mine, given = lax.optimization_barrier((mine, given))
                    weight_grad = gather_y_core(mine) * (1.0 / math.sqrt(node_total))
            x_grads.append((kept + row_permute(given, zh=1).astype(F32)).astype(BF16))
    x_grad = jnp.concatenate(x_grads, axis=1)

    return (activation, weight_grad, x_grad)


def solution(mesh):
    return jax.shard_map(
        local,
        mesh=mesh,
        in_specs=(
            P(("col", "row"), None),
            P("row", "col", None, None, None),
            P("row", "col", None),
            P("row", "col", None),
            P("row", "col"),
            P(),
            P(("row", "col"), None),
        ),
        out_specs=(P(("row", "col"), None), P(), P(("col", "row"), None)),
        check_vma=False,
    )
```

```python
import functools
import math

import jax
import jax.numpy as jnp
from jax import lax
from jax.experimental import pallas as pl
from jax.experimental.pallas import tpu as pltpu
from jax.sharding import PartitionSpec as P

ROW_DEVICES = 16
COL_DEVICES = 16
UNROLL = 4
EDGE = 256
HALF = 128
GROUP = 4 * EDGE
WEIGHT_ROWS = 128
VMEM_BYTES = 48 << 20
BF16 = jnp.bfloat16
F32 = jnp.float32


def row_permute(value, zh=0, y=0, core=0):
    pairs = []
    for i in range(ROW_DEVICES):
        to_zh, to_y, to_core = (i >> 3) ^ zh, (((i >> 1) & 3) + y) % 4, (i & 1) ^ core
        pairs.append((i, (to_zh * 4 + to_y) * 2 + to_core))
    return lax.ppermute(value, "row", pairs)


def col_permute(value, x=0, zl=0):
    pairs = []
    for i in range(COL_DEVICES):
        pairs.append((i, (((i >> 2) + x) % 4) * 4 + ((i & 3) + zl) % 4))
    return lax.ppermute(value, "col", pairs)


def row_tile(k, j, flip):
    index = lax.axis_index("row")
    zh, y, core = index >> 3, (index >> 1) & 3, index & 1
    return ((zh ^ j) * 4 + ((y + k) & 3)) * 2 + (core ^ flip)


def col_tile(k, j):
    index = lax.axis_index("col")
    return (((index >> 2) + k) & 3) * 4 + ((index + j) & 3)


def tile_loop(count, into, frm, tiles, panel, tile_buf, acc, tile_sem, piece_copies, contract):
    @pl.loop(0, count)
    def _(i):
        pltpu.make_async_copy(tiles.at[i], tile_buf.at[i], tile_sem.at[i]).start()

    for copy in piece_copies:
        copy.start()

    @pl.loop(0, acc.shape[0])
    def _(i):
        acc[i] = jnp.zeros(acc.shape[1:], F32)

    for copy in piece_copies:
        copy.wait()

    def arrive(i):
        pltpu.make_async_copy(tiles.at[i], tile_buf.at[i], tile_sem.at[i]).wait()

    def product(i):
        return lax.dot_general(
            tile_buf[i], panel[frm[i]], (((contract,), (0,)), ((), ())), preferred_element_type=F32
        )

    groups = count // UNROLL

    @pl.loop(0, groups)
    def _(group):
        first = group * UNROLL
        for j in range(UNROLL):
            arrive(first + j)
        terms = [product(first + j) for j in range(UNROLL)]
        for j in range(UNROLL):
            acc[into[first + j]] += terms[j]

    @pl.loop(groups * UNROLL, count)
    def _(i):
        arrive(i)
        acc[into[i]] += product(i)


def forward_kernel(cnt, into, frm, near, far, tiles, o0, o1, o2, o3, panel, tile_buf, acc, tile_sem, piece_sem):
    copies = []
    for flip, piece in enumerate((near, far)):
        for k in range(4):
            for j in range(2):
                n = k * 2 + j
                copies.append(
                    pltpu.make_async_copy(
                        piece.at[n], panel.at[row_tile(-k, j, flip)], piece_sem.at[flip * 8 + n]
                    )
                )
    tile_loop(cnt[0], into, frm, tiles, panel, tile_buf, acc, tile_sem, copies, 1)
    for k, out in enumerate((o0, o1, o2, o3)):
        for j in range(4):
            out[j] = acc[col_tile(k, j)].astype(BF16)


def backward_kernel(with_weight, cnt, into, frm, g0, g1, g2, g3, tiles, *refs):
    if with_weight:
        own, sent, panel, tile_buf, acc, tile_sem, piece_sem, weight_buf = refs
    else:
        own, sent, panel, tile_buf, acc, tile_sem, piece_sem = refs
    copies = []
    for k, piece in enumerate((g0, g1, g2, g3)):
        for j in range(4):
            copies.append(
                pltpu.make_async_copy(
                    piece.at[pl.ds(j * EDGE, EDGE)], panel.at[col_tile(-k, -j)], piece_sem.at[k * 4 + j]
                )
            )
    if with_weight:
        for k, piece in enumerate((g0, g1, g2, g3)):
            copies.append(
                pltpu.make_async_copy(
                    piece.at[pl.ds(GROUP, WEIGHT_ROWS)], weight_buf.at[k], piece_sem.at[16 + k]
                )
            )
    tile_loop(cnt[0], into, frm, tiles, panel, tile_buf, acc, tile_sem, copies, 0)
    if with_weight:
        x = lax.axis_index("col") >> 2
        term = weight_buf[x].astype(F32)
        for place in range(1, 4):
            term = term + weight_buf[(x - place) & 3].astype(F32)
        term = term.astype(BF16)
    for flip, out in enumerate((own, sent)):
        for k in range(4):
            for j in range(2):
                out[k, j * EDGE : (j + 1) * EDGE] = acc[row_tile(k, j, flip)].astype(BF16)
            if with_weight:
                out[k, 2 * EDGE :] = term


def tile_call(kernel, name, cnt, into, frm, pieces, tiles, out_shapes, with_weight=False):
    slots, edge, _ = tiles.shape
    smem = pl.BlockSpec(memory_space=pltpu.SMEM)
    hbm = pl.BlockSpec(memory_space=pl.ANY)
    vmem = pl.BlockSpec(memory_space=pltpu.VMEM)
    scratch = [
        pltpu.VMEM((16, edge, HALF), BF16),
        pltpu.VMEM((slots, edge, edge), BF16),
        pltpu.VMEM((16, edge, HALF), F32),
        pltpu.SemaphoreType.DMA((slots,)),
        pltpu.SemaphoreType.DMA((20,)),
    ]
    if with_weight:
        scratch.append(pltpu.VMEM((4, WEIGHT_ROWS, HALF), BF16))
    return pl.pallas_call(
        kernel,
        out_shape=[jax.ShapeDtypeStruct(shape, BF16) for shape in out_shapes],
        in_specs=[smem] * 3 + [hbm] * (len(pieces) + 1),
        out_specs=[vmem] * len(out_shapes),
        scratch_shapes=scratch,
        compiler_params=pltpu.CompilerParams(vmem_limit_bytes=VMEM_BYTES),
        cost_estimate=pl.CostEstimate(
            flops=2 * slots * edge**3, bytes_accessed=slots * edge * edge * 2, transcendentals=0
        ),
        name=name,
    )(cnt, into, frm, *pieces, tiles)


def small_call(kernel, name, out_shapes, operands, scratch=(), flops=10**6):
    return pl.pallas_call(
        kernel,
        out_shape=[jax.ShapeDtypeStruct(shape, dtype) for shape, dtype in out_shapes],
        scratch_shapes=list(scratch),
        compiler_params=pltpu.CompilerParams(vmem_limit_bytes=8 << 20),
        cost_estimate=pl.CostEstimate(flops=flops, bytes_accessed=10**6, transcendentals=0),
        name=name,
    )(*operands)


def dense_kernel(*refs):
    quads, (weight, grad_out, activation, weight_own, m0, z1, z2, z3, m1, term) = refs[:8], refs[8:]
    aggregated = []
    for own, q1, q2, q3 in (quads[:4], quads[4:]):
        total = own[...] + q1[...].astype(F32) + q2[...].astype(F32) + q3[...].astype(F32)
        aggregated.append(total.astype(BF16))
    pre_act = jnp.dot(aggregated[0], weight[:HALF], preferred_element_type=F32)
    pre_act += jnp.dot(aggregated[1], weight[HALF:], preferred_element_type=F32)
    gate_sig = 1.0 / (1.0 + jnp.exp(-pre_act))
    activation[...] = (pre_act * gate_sig).astype(BF16)
    slope = gate_sig * (1.0 + pre_act * (1.0 - gate_sig))
    act_grad = (grad_out[...].astype(F32) * slope).astype(BF16)
    msg_grad = lax.dot_general(
        act_grad, weight[...], (((1,), (1,)), ((), ())), preferred_element_type=F32
    ).astype(BF16)
    for out in (m0, z1, z2, z3):
        out[:EDGE] = msg_grad[:, :HALF]
    m1[...] = msg_grad[:, HALF:]
    for part in range(2):
        term[part * HALF : (part + 1) * HALF] = lax.dot_general(
            aggregated[part], act_grad, (((0,), (0,)), ((), ())), preferred_element_type=F32
        )
    zl = lax.axis_index("col") & 3
    for k, (out, base) in enumerate(((weight_own, 0), (z1, EDGE), (z2, EDGE), (z3, EDGE))):
        rows = pl.ds(pl.multiple_of(((zl + k) & 3) * 64, 64), 64)
        for side in range(2):
            first = base + side * 64
            out[first : first + 64] = term[rows, side * HALF : (side + 1) * HALF].astype(out.dtype)


def dense_call(sums, weight, grad_out):
    return small_call(
        dense_kernel,
        "dense",
        [(grad_out.shape, BF16), ((HALF, HALF), F32), ((EDGE, HALF), BF16)]
        + [((EDGE + HALF, HALF), BF16)] * 3
        + [((EDGE, HALF), BF16)],
        (*sums, weight, grad_out),
        [pltpu.VMEM((EDGE, EDGE), F32)],
        6 * 256**3,
    )


def pack_kernel(m0, z1, z2, z3, weight_own, group):
    term = weight_own[...]
    for piece in (z1, z2, z3):
        term = term + piece[EDGE:].astype(F32)
    for j, piece in enumerate((m0, z1, z2, z3)):
        group[j * EDGE : (j + 1) * EDGE] = piece[:EDGE]
    group[GROUP:] = term.astype(BF16)


def pack_call(m0, received, weight_own):
    return small_call(
        pack_kernel,
        "pack_messages",
        [((GROUP + WEIGHT_ROWS, HALF), BF16)],
        (m0, *received, weight_own),
    )[0]


def add_y_kernel(q0, q1, q2, q3, kept, given, buf):
    quads = (q0, q1, q2, q3)
    total = quads[0][...].astype(F32)
    for quad in quads[1:]:
        total = total + quad[...].astype(F32)
    kept[...] = total[:EDGE]
    given[:EDGE] = total[EDGE : 2 * EDGE].astype(BF16)
    if given.shape[0] > EDGE:
        for k, quad in enumerate(quads):
            buf[k] = quad[2 * EDGE :].astype(F32)
        y = (lax.axis_index("row") >> 1) & 3
        term = buf[y]
        for place in range(1, 4):
            term = term + buf[(y - place) & 3]
        given[EDGE:] = term.astype(BF16)


def add_y_call(quads):
    rows = quads[0].shape[0]
    return small_call(
        add_y_kernel,
        "add_over_y",
        [((EDGE, HALF), F32), ((rows - EDGE, HALF), BF16)],
        quads,
        [pltpu.VMEM((4, WEIGHT_ROWS, HALF), F32)],
    )


def spread_kernel(scale, a0, a1, a2, a3, out):
    col = lax.axis_index("col")
    for k, piece in enumerate((a0, a1, a2, a3)):
        row = pl.multiple_of(((col - k) & 3) * 64, 64)
        for side in range(2):
            out[pl.ds(row, 64), side * HALF : (side + 1) * HALF] = piece[side * 64 : side * 64 + 64] * scale


def add_all(pieces):
    total = pieces[0].astype(F32)
    for piece in pieces[1:]:
        total = total + piece.astype(F32)
    return total


def local(features, adj_tiles, tile_rows, tile_cols, tile_count, weight, grad_out):
    tiles = adj_tiles[0, 0]
    row_ids, col_ids, count = tile_rows[0, 0], tile_cols[0, 0], tile_count[0]
    node_total = EDGE * ROW_DEVICES * COL_DEVICES

    with jax.named_scope("gather_features"):
        other = row_permute(features, zh=1)
        pairs = [
            jnp.stack([value[:, h * HALF : (h + 1) * HALF] for value in (features, other)]) for h in range(2)
        ]
    for h in range(2):
        with jax.named_scope("gather_features"):
            near = jnp.concatenate([pairs[h]] + [row_permute(pairs[h], y=k) for k in (1, 2, 3)])
            if h == 1:
                near, before = lax.optimization_barrier((near, parts))
            far = row_permute(near, core=1)
            if h == 0:
                far, pairs[1] = lax.optimization_barrier((far, pairs[1]))
        parts = tile_call(
            forward_kernel, "forward_tiles", count, row_ids, col_ids, [near, far], tiles, [(4, EDGE, HALF)] * 4
        )
    sums = []
    for parts in (before, parts):
        with jax.named_scope("reduce_aggregate"):
            parts = [parts[0]] + [col_permute(parts[k], x=k) for k in (1, 2, 3)]
            part_sums = [add_all([part[j] for part in parts]) for j in range(4)]
            sums += [part_sums[0]] + [col_permute(part_sums[k].astype(BF16), zl=k) for k in (1, 2, 3)]

    activation, weight_own, m0, z1, z2, z3, m1 = dense_call(sums, weight, grad_out)

    with jax.named_scope("gather_messages"):
        arrived = [col_permute(z, zl=k) for k, z in ((1, z1), (2, z2), (3, z3))]
        group = pack_call(m0, arrived, weight_own)
        first = [group] + [col_permute(group, x=k) for k in (1, 2, 3)]
        group = jnp.concatenate([m1] + [col_permute(m1, zl=k) for k in (1, 2, 3)])
        first, group = lax.optimization_barrier((first, group))
        second = [group] + [col_permute(group, x=k) for k in (1, 2, 3)]

    kept, given = [None, None], [None, None]
    for h, group in enumerate((first, second)):
        if h == 1:
            group, given[0] = lax.optimization_barrier((group, given[0]))
        rows = 2 * EDGE + (WEIGHT_ROWS if h == 0 else 0)
        own, sent = tile_call(
            functools.partial(backward_kernel, h == 0),
            "backward_tiles",
            count,
            col_ids,
            row_ids,
            group,
            tiles,
            [(4, rows, HALF)] * 2,
            h == 0,
        )
        if h == 1:
            with jax.named_scope("reduce_features"):
                first = row_permute(given[0], zh=1)
            own, sent, first = lax.optimization_barrier((own, sent, first))
        with jax.named_scope("reduce_features"):
            both = add_all([own, row_permute(sent, core=1)]).astype(BF16)
            quads = [both[0]] + [row_permute(both[k], y=k) for k in (1, 2, 3)]
            kept[h], given[h] = add_y_call(quads)
    with jax.named_scope("reduce_features"):
        last = [first, row_permute(given[1], zh=1)]
        halves = [mine + theirs[:EDGE].astype(F32) for mine, theirs in zip(kept, last)]
    with jax.named_scope("gather_weight"):
        mine = given[0][EDGE:].astype(F32) + last[0][EDGE:].astype(F32)
        mine = [mine] + [col_permute(mine, zl=k) for k in (1, 2, 3)]
    x_grad = jnp.concatenate(halves, axis=1).astype(BF16)
    weight_grad = small_call(
        functools.partial(spread_kernel, 1.0 / math.sqrt(node_total)), "spread_weight", [((EDGE, EDGE), F32)], mine
    )[0]

    return (activation, weight_grad, x_grad)


def solution(mesh):
    return jax.shard_map(
        local,
        mesh=mesh,
        in_specs=(
            P(("col", "row"), None),
            P("row", "col", None, None, None),
            P("row", "col", None),
            P("row", "col", None),
            P("row", "col"),
            P(),
            P(("row", "col"), None),
        ),
        out_specs=(P(("row", "col"), None), P(), P(("col", "row"), None)),
        check_vma=False,
    )
```

```python
import functools
import math

import jax
import jax.numpy as jnp
from jax import lax
from jax.experimental import pallas as pl
from jax.experimental.pallas import tpu as pltpu
from jax.sharding import PartitionSpec as P

ROW_DEVICES = 16
COL_DEVICES = 16
UNROLLS = (16, 4, 1)
EDGE = 256
HALF = 128
GROUP = 4 * EDGE
WEIGHT_ROWS = 128
VMEM_BYTES = 48 << 20
BF16 = jnp.bfloat16
F32 = jnp.float32


def row_permute(value, zh=0, y=0, core=0):
    pairs = []
    for i in range(ROW_DEVICES):
        to_zh, to_y, to_core = (i >> 3) ^ zh, (((i >> 1) & 3) + y) % 4, (i & 1) ^ core
        pairs.append((i, (to_zh * 4 + to_y) * 2 + to_core))
    return lax.ppermute(value, "row", pairs)


def col_permute(value, x=0, zl=0):
    pairs = []
    for i in range(COL_DEVICES):
        pairs.append((i, (((i >> 2) + x) % 4) * 4 + ((i & 3) + zl) % 4))
    return lax.ppermute(value, "col", pairs)


def row_tile(k, j, flip):
    index = lax.axis_index("row")
    zh, y, core = index >> 3, (index >> 1) & 3, index & 1
    return ((zh ^ j) * 4 + ((y + k) & 3)) * 2 + (core ^ flip)


def col_tile(k, j):
    index = lax.axis_index("col")
    return (((index >> 2) + k) & 3) * 4 + ((index + j) & 3)


def tile_loop(count, into, frm, tiles, panel, tile_buf, acc, tile_sem, piece_copies, contract):
    @pl.loop(0, count)
    def _(i):
        pltpu.make_async_copy(tiles.at[i], tile_buf.at[i], tile_sem.at[i]).start()

    for copy in piece_copies:
        copy.start()

    @pl.loop(0, acc.shape[0])
    def _(i):
        acc[i] = jnp.zeros(acc.shape[1:], F32)

    for copy in piece_copies:
        copy.wait()

    def arrive(i):
        pltpu.make_async_copy(tiles.at[i], tile_buf.at[i], tile_sem.at[i]).wait()

    def product(i):
        return lax.dot_general(
            tile_buf[i], panel[frm[i]], (((contract,), (0,)), ((), ())), preferred_element_type=F32
        )

    done = 0
    for size in UNROLLS:
        groups = (count - done) // size

        @pl.loop(0, groups)
        def _(group, done=done, size=size):
            first = done + group * size
            for j in range(size):
                arrive(first + j)
            terms = [product(first + j) for j in range(size)]
            for j in range(size):
                acc[into[first + j]] += terms[j]

        done = done + groups * size


def forward_kernel(cnt, into, frm, near, far, tiles, o0, o1, o2, o3, panel, tile_buf, acc, tile_sem, piece_sem):
    copies = []
    for flip, piece in enumerate((near, far)):
        for k in range(4):
            for j in range(2):
                n = k * 2 + j
                copies.append(
                    pltpu.make_async_copy(
                        piece.at[n], panel.at[row_tile(-k, j, flip)], piece_sem.at[flip * 8 + n]
                    )
                )
    tile_loop(cnt[0], into, frm, tiles, panel, tile_buf, acc, tile_sem, copies, 1)
    for k, out in enumerate((o0, o1, o2, o3)):
        for j in range(4):
            out[j] = acc[col_tile(k, j)].astype(BF16)


def backward_kernel(with_weight, cnt, into, frm, g0, g1, g2, g3, tiles, *refs):
    if with_weight:
        own, sent, panel, tile_buf, acc, tile_sem, piece_sem, weight_buf = refs
    else:
        own, sent, panel, tile_buf, acc, tile_sem, piece_sem = refs
    copies = []
    for k, piece in enumerate((g0, g1, g2, g3)):
        for j in range(4):
            copies.append(
                pltpu.make_async_copy(
                    piece.at[pl.ds(j * EDGE, EDGE)], panel.at[col_tile(-k, -j)], piece_sem.at[k * 4 + j]
                )
            )
    if with_weight:
        for k, piece in enumerate((g0, g1, g2, g3)):
            copies.append(
                pltpu.make_async_copy(
                    piece.at[pl.ds(GROUP, WEIGHT_ROWS)], weight_buf.at[k], piece_sem.at[16 + k]
                )
            )
    tile_loop(cnt[0], into, frm, tiles, panel, tile_buf, acc, tile_sem, copies, 0)
    if with_weight:
        x = lax.axis_index("col") >> 2
        term = weight_buf[x].astype(F32)
        for place in range(1, 4):
            term = term + weight_buf[(x - place) & 3].astype(F32)
        term = term.astype(BF16)
    for flip, out in enumerate((own, sent)):
        for k in range(4):
            for j in range(2):
                out[k, j * EDGE : (j + 1) * EDGE] = acc[row_tile(k, j, flip)].astype(BF16)
            if with_weight:
                out[k, 2 * EDGE :] = term


def tile_call(kernel, name, cnt, into, frm, pieces, tiles, out_shapes, with_weight=False):
    slots, edge, _ = tiles.shape
    smem = pl.BlockSpec(memory_space=pltpu.SMEM)
    hbm = pl.BlockSpec(memory_space=pl.ANY)
    vmem = pl.BlockSpec(memory_space=pltpu.VMEM)
    scratch = [
        pltpu.VMEM((16, edge, HALF), BF16),
        pltpu.VMEM((slots, edge, edge), BF16),
        pltpu.VMEM((16, edge, HALF), F32),
        pltpu.SemaphoreType.DMA((slots,)),
        pltpu.SemaphoreType.DMA((20,)),
    ]
    if with_weight:
        scratch.append(pltpu.VMEM((4, WEIGHT_ROWS, HALF), BF16))
    return pl.pallas_call(
        kernel,
        out_shape=[jax.ShapeDtypeStruct(shape, BF16) for shape in out_shapes],
        in_specs=[smem] * 3 + [hbm] * (len(pieces) + 1),
        out_specs=[vmem] * len(out_shapes),
        scratch_shapes=scratch,
        compiler_params=pltpu.CompilerParams(vmem_limit_bytes=VMEM_BYTES),
        cost_estimate=pl.CostEstimate(
            flops=2 * slots * edge**3, bytes_accessed=slots * edge * edge * 2, transcendentals=0
        ),
        name=name,
    )(cnt, into, frm, *pieces, tiles)


def small_call(kernel, name, out_shapes, operands, scratch=(), flops=10**6):
    return pl.pallas_call(
        kernel,
        out_shape=[jax.ShapeDtypeStruct(shape, dtype) for shape, dtype in out_shapes],
        scratch_shapes=list(scratch),
        compiler_params=pltpu.CompilerParams(vmem_limit_bytes=8 << 20),
        cost_estimate=pl.CostEstimate(flops=flops, bytes_accessed=10**6, transcendentals=0),
        name=name,
    )(*operands)


def dense_kernel(*refs):
    quads, (weight, grad_out, activation, weight_own, m0, z1, z2, z3, m1, term) = refs[:8], refs[8:]
    aggregated = []
    for own, q1, q2, q3 in (quads[:4], quads[4:]):
        total = own[...] + q1[...].astype(F32) + q2[...].astype(F32) + q3[...].astype(F32)
        aggregated.append(total.astype(BF16))
    pre_act = jnp.dot(aggregated[0], weight[:HALF], preferred_element_type=F32)
    pre_act += jnp.dot(aggregated[1], weight[HALF:], preferred_element_type=F32)
    gate_sig = 1.0 / (1.0 + jnp.exp(-pre_act))
    activation[...] = (pre_act * gate_sig).astype(BF16)
    slope = gate_sig * (1.0 + pre_act * (1.0 - gate_sig))
    act_grad = (grad_out[...].astype(F32) * slope).astype(BF16)
    msg_grad = lax.dot_general(
        act_grad, weight[...], (((1,), (1,)), ((), ())), preferred_element_type=F32
    ).astype(BF16)
    for out in (m0, z1, z2, z3):
        out[:EDGE] = msg_grad[:, :HALF]
    m1[...] = msg_grad[:, HALF:]
    for part in range(2):
        term[part * HALF : (part + 1) * HALF] = lax.dot_general(
            aggregated[part], act_grad, (((0,), (0,)), ((), ())), preferred_element_type=F32
        )
    zl = lax.axis_index("col") & 3
    for k, (out, base) in enumerate(((weight_own, 0), (z1, EDGE), (z2, EDGE), (z3, EDGE))):
        rows = pl.ds(pl.multiple_of(((zl + k) & 3) * 64, 64), 64)
        for side in range(2):
            first = base + side * 64
            out[first : first + 64] = term[rows, side * HALF : (side + 1) * HALF].astype(out.dtype)


def dense_call(sums, weight, grad_out):
    return small_call(
        dense_kernel,
        "dense",
        [(grad_out.shape, BF16), ((HALF, HALF), F32), ((EDGE, HALF), BF16)]
        + [((EDGE + HALF, HALF), BF16)] * 3
        + [((EDGE, HALF), BF16)],
        (*sums, weight, grad_out),
        [pltpu.VMEM((EDGE, EDGE), F32)],
        6 * 256**3,
    )


def pack_kernel(m0, z1, z2, z3, weight_own, group):
    term = weight_own[...]
    for piece in (z1, z2, z3):
        term = term + piece[EDGE:].astype(F32)
    for j, piece in enumerate((m0, z1, z2, z3)):
        group[j * EDGE : (j + 1) * EDGE] = piece[:EDGE]
    group[GROUP:] = term.astype(BF16)


def pack_call(m0, received, weight_own):
    return small_call(
        pack_kernel,
        "pack_messages",
        [((GROUP + WEIGHT_ROWS, HALF), BF16)],
        (m0, *received, weight_own),
    )[0]


def add_y_kernel(q0, q1, q2, q3, kept, given, buf):
    quads = (q0, q1, q2, q3)
    total = quads[0][...].astype(F32)
    for quad in quads[1:]:
        total = total + quad[...].astype(F32)
    kept[...] = total[:EDGE]
    given[:EDGE] = total[EDGE : 2 * EDGE].astype(BF16)
    if given.shape[0] > EDGE:
        for k, quad in enumerate(quads):
            buf[k] = quad[2 * EDGE :].astype(F32)
        y = (lax.axis_index("row") >> 1) & 3
        term = buf[y]
        for place in range(1, 4):
            term = term + buf[(y - place) & 3]
        given[EDGE:] = term.astype(BF16)


def add_y_call(quads):
    rows = quads[0].shape[0]
    return small_call(
        add_y_kernel,
        "add_over_y",
        [((EDGE, HALF), F32), ((rows - EDGE, HALF), BF16)],
        quads,
        [pltpu.VMEM((4, WEIGHT_ROWS, HALF), F32)],
    )


def spread_kernel(scale, a0, a1, a2, a3, out):
    col = lax.axis_index("col")
    for k, piece in enumerate((a0, a1, a2, a3)):
        row = pl.multiple_of(((col - k) & 3) * 64, 64)
        for side in range(2):
            out[pl.ds(row, 64), side * HALF : (side + 1) * HALF] = piece[side * 64 : side * 64 + 64] * scale


def add_all(pieces):
    total = pieces[0].astype(F32)
    for piece in pieces[1:]:
        total = total + piece.astype(F32)
    return total


def local(features, adj_tiles, tile_rows, tile_cols, tile_count, weight, grad_out):
    tiles = adj_tiles[0, 0]
    row_ids, col_ids, count = tile_rows[0, 0], tile_cols[0, 0], tile_count[0]
    node_total = EDGE * ROW_DEVICES * COL_DEVICES

    with jax.named_scope("gather_features"):
        other = row_permute(features, zh=1)
        pairs = [
            jnp.stack([value[:, h * HALF : (h + 1) * HALF] for value in (features, other)]) for h in range(2)
        ]
    for h in range(2):
        with jax.named_scope("gather_features"):
            near = jnp.concatenate([pairs[h]] + [row_permute(pairs[h], y=k) for k in (1, 2, 3)])
            if h == 1:
                near, before = lax.optimization_barrier((near, parts))
            far = row_permute(near, core=1)
            if h == 0:
                far, pairs[1] = lax.optimization_barrier((far, pairs[1]))
        parts = tile_call(
            forward_kernel, "forward_tiles", count, row_ids, col_ids, [near, far], tiles, [(4, EDGE, HALF)] * 4
        )
    sums = []
    for parts in (before, parts):
        with jax.named_scope("reduce_aggregate"):
            parts = [parts[0]] + [col_permute(parts[k], x=k) for k in (1, 2, 3)]
            part_sums = [add_all([part[j] for part in parts]) for j in range(4)]
            sums += [part_sums[0]] + [col_permute(part_sums[k].astype(BF16), zl=k) for k in (1, 2, 3)]

    activation, weight_own, m0, z1, z2, z3, m1 = dense_call(sums, weight, grad_out)

    with jax.named_scope("gather_messages"):
        arrived = [col_permute(z, zl=k) for k, z in ((1, z1), (2, z2), (3, z3))]
        group = pack_call(m0, arrived, weight_own)
        first = [group] + [col_permute(group, x=k) for k in (1, 2, 3)]
        group = jnp.concatenate([m1] + [col_permute(m1, zl=k) for k in (1, 2, 3)])
        first, group = lax.optimization_barrier((first, group))
        second = [group] + [col_permute(group, x=k) for k in (1, 2, 3)]

    def products(h, group):
        return tile_call(
            functools.partial(backward_kernel, h == 0),
            "backward_tiles",
            count,
            col_ids,
            row_ids,
            group,
            tiles,
            [(4, 2 * EDGE + (WEIGHT_ROWS if h == 0 else 0), HALF)] * 2,
            h == 0,
        )

    def add_core(own, sent):
        both = add_all([own, row_permute(sent, core=1)]).astype(BF16)
        return [both[0]] + [row_permute(both[k], y=k) for k in (1, 2, 3)]

    own, sent = products(0, first)
    beside = [1, 3]
    own, sent, arrived = lax.optimization_barrier((own, sent, [second[k] for k in beside]))
    for k, value in zip(beside, arrived):
        second[k] = value
    with jax.named_scope("reduce_features"):
        quads = add_core(own, sent)
    own, sent = products(1, second)
    own, sent, quads = lax.optimization_barrier((own, sent, quads))
    with jax.named_scope("reduce_features"):
        kept0, given0 = add_y_call(quads)
        last0 = row_permute(given0, zh=1)
        kept1, given1 = add_y_call(add_core(own, sent))
        last1 = row_permute(given1, zh=1)
        halves = [kept0 + last0[:EDGE].astype(F32), kept1 + last1.astype(F32)]
    with jax.named_scope("gather_weight"):
        mine = given0[EDGE:].astype(F32) + last0[EDGE:].astype(F32)
        mine = [mine] + [col_permute(mine, zl=k) for k in (1, 2, 3)]
    x_grad = jnp.concatenate(halves, axis=1).astype(BF16)
    weight_grad = small_call(
        functools.partial(spread_kernel, 1.0 / math.sqrt(node_total)), "spread_weight", [((EDGE, EDGE), F32)], mine
    )[0]

    return (activation, weight_grad, x_grad)


def solution(mesh):
    return jax.shard_map(
        local,
        mesh=mesh,
        in_specs=(
            P(("col", "row"), None),
            P("row", "col", None, None, None),
            P("row", "col", None),
            P("row", "col", None),
            P("row", "col"),
            P(),
            P(("row", "col"), None),
        ),
        out_specs=(P(("row", "col"), None), P(), P(("col", "row"), None)),
        check_vma=False,
    )
```

```python
import functools
import math

import jax
import jax.numpy as jnp
from jax import lax
from jax.experimental import pallas as pl
from jax.experimental.pallas import tpu as pltpu
from jax.sharding import PartitionSpec as P

ROW_DEVICES = 16
COL_DEVICES = 16
UNROLLS = (32, 16, 4, 1)
EDGE = 256
HALF = 128
GROUP = 4 * EDGE
WEIGHT_ROWS = 128
VMEM_BYTES = 48 << 20
BF16 = jnp.bfloat16
F32 = jnp.float32


def row_permute(value, zh=0, y=0, core=0):
    pairs = []
    for i in range(ROW_DEVICES):
        to_zh, to_y, to_core = (i >> 3) ^ zh, (((i >> 1) & 3) + y) % 4, (i & 1) ^ core
        pairs.append((i, (to_zh * 4 + to_y) * 2 + to_core))
    return lax.ppermute(value, "row", pairs)


def col_permute(value, x=0, zl=0):
    pairs = []
    for i in range(COL_DEVICES):
        pairs.append((i, (((i >> 2) + x) % 4) * 4 + ((i & 3) + zl) % 4))
    return lax.ppermute(value, "col", pairs)


def row_tile(k, j, flip):
    index = lax.axis_index("row")
    zh, y, core = index >> 3, (index >> 1) & 3, index & 1
    return ((zh ^ j) * 4 + ((y + k) & 3)) * 2 + (core ^ flip)


def col_tile(k, j):
    index = lax.axis_index("col")
    return (((index >> 2) + k) & 3) * 4 + ((index + j) & 3)


def tile_loop(count, into, frm, tiles, panel, tile_buf, acc, tile_sem, piece_copies, contract):
    @pl.loop(0, count)
    def _(i):
        pltpu.make_async_copy(tiles.at[i], tile_buf.at[i], tile_sem.at[i]).start()

    for copy in piece_copies:
        copy.start()

    @pl.loop(0, acc.shape[0])
    def _(i):
        acc[i] = jnp.zeros(acc.shape[1:], F32)

    for copy in piece_copies:
        copy.wait()

    def arrive(i):
        pltpu.make_async_copy(tiles.at[i], tile_buf.at[i], tile_sem.at[i]).wait()

    def product(i):
        return lax.dot_general(
            tile_buf[i], panel[frm[i]], (((contract,), (0,)), ((), ())), preferred_element_type=F32
        )

    done = 0
    for size in UNROLLS:
        groups = (count - done) // size

        @pl.loop(0, groups)
        def _(group, done=done, size=size):
            first = done + group * size
            for j in range(size):
                arrive(first + j)
            terms = [product(first + j) for j in range(size)]
            for j in range(size):
                acc[into[first + j]] += terms[j]

        done = done + groups * size


def forward_kernel(cnt, into, frm, near, far, tiles, o0, o1, o2, o3, panel, tile_buf, acc, tile_sem, piece_sem):
    copies = []
    for flip, piece in enumerate((near, far)):
        for k in range(4):
            for j in range(2):
                n = k * 2 + j
                copies.append(
                    pltpu.make_async_copy(
                        piece.at[n], panel.at[row_tile(-k, j, flip)], piece_sem.at[flip * 8 + n]
                    )
                )
    tile_loop(cnt[0], into, frm, tiles, panel, tile_buf, acc, tile_sem, copies, 1)
    for k, out in enumerate((o0, o1, o2, o3)):
        for j in range(4):
            out[j] = acc[col_tile(k, j)].astype(BF16)


def backward_kernel(with_weight, cnt, into, frm, g0, g1, g2, g3, tiles, *refs):
    if with_weight:
        own, sent, panel, tile_buf, acc, tile_sem, piece_sem, weight_buf = refs
    else:
        own, sent, panel, tile_buf, acc, tile_sem, piece_sem = refs
    copies = []
    for k, piece in enumerate((g0, g1, g2, g3)):
        for j in range(4):
            copies.append(
                pltpu.make_async_copy(
                    piece.at[pl.ds(j * EDGE, EDGE)], panel.at[col_tile(-k, -j)], piece_sem.at[k * 4 + j]
                )
            )
    if with_weight:
        for k, piece in enumerate((g0, g1, g2, g3)):
            copies.append(
                pltpu.make_async_copy(
                    piece.at[pl.ds(GROUP, WEIGHT_ROWS)], weight_buf.at[k], piece_sem.at[16 + k]
                )
            )
    tile_loop(cnt[0], into, frm, tiles, panel, tile_buf, acc, tile_sem, copies, 0)
    if with_weight:
        x = lax.axis_index("col") >> 2
        term = weight_buf[x].astype(F32)
        for place in range(1, 4):
            term = term + weight_buf[(x - place) & 3].astype(F32)
        term = term.astype(BF16)
    for flip, out in enumerate((own, sent)):
        for k in range(4):
            for j in range(2):
                out[k, j * EDGE : (j + 1) * EDGE] = acc[row_tile(k, j, flip)].astype(BF16)
            if with_weight:
                out[k, 2 * EDGE :] = term


def tile_call(kernel, name, cnt, into, frm, pieces, tiles, out_shapes, with_weight=False):
    slots, edge, _ = tiles.shape
    smem = pl.BlockSpec(memory_space=pltpu.SMEM)
    hbm = pl.BlockSpec(memory_space=pl.ANY)
    vmem = pl.BlockSpec(memory_space=pltpu.VMEM)
    scratch = [
        pltpu.VMEM((16, edge, HALF), BF16),
        pltpu.VMEM((slots, edge, edge), BF16),
        pltpu.VMEM((16, edge, HALF), F32),
        pltpu.SemaphoreType.DMA((slots,)),
        pltpu.SemaphoreType.DMA((20,)),
    ]
    if with_weight:
        scratch.append(pltpu.VMEM((4, WEIGHT_ROWS, HALF), BF16))
    return pl.pallas_call(
        kernel,
        out_shape=[jax.ShapeDtypeStruct(shape, BF16) for shape in out_shapes],
        in_specs=[smem] * 3 + [hbm] * (len(pieces) + 1),
        out_specs=[vmem] * len(out_shapes),
        scratch_shapes=scratch,
        compiler_params=pltpu.CompilerParams(vmem_limit_bytes=VMEM_BYTES),
        cost_estimate=pl.CostEstimate(
            flops=2 * slots * edge**3, bytes_accessed=slots * edge * edge * 2, transcendentals=0
        ),
        name=name,
    )(cnt, into, frm, *pieces, tiles)


def small_call(kernel, name, out_shapes, operands, scratch=(), flops=10**6):
    return pl.pallas_call(
        kernel,
        out_shape=[jax.ShapeDtypeStruct(shape, dtype) for shape, dtype in out_shapes],
        scratch_shapes=list(scratch),
        compiler_params=pltpu.CompilerParams(vmem_limit_bytes=8 << 20),
        cost_estimate=pl.CostEstimate(flops=flops, bytes_accessed=10**6, transcendentals=0),
        name=name,
    )(*operands)


def dense_kernel(*refs):
    quads, (weight, grad_out, activation, weight_own, m0, z1, z2, z3, m1, term) = refs[:8], refs[8:]
    aggregated = []
    for own, q1, q2, q3 in (quads[:4], quads[4:]):
        total = own[...] + q1[...].astype(F32) + q2[...].astype(F32) + q3[...].astype(F32)
        aggregated.append(total.astype(BF16))
    pre_act = jnp.dot(aggregated[0], weight[:HALF], preferred_element_type=F32)
    pre_act += jnp.dot(aggregated[1], weight[HALF:], preferred_element_type=F32)
    gate_sig = 1.0 / (1.0 + jnp.exp(-pre_act))
    activation[...] = (pre_act * gate_sig).astype(BF16)
    slope = gate_sig * (1.0 + pre_act * (1.0 - gate_sig))
    act_grad = (grad_out[...].astype(F32) * slope).astype(BF16)
    msg_grad = lax.dot_general(
        act_grad, weight[...], (((1,), (1,)), ((), ())), preferred_element_type=F32
    ).astype(BF16)
    for out in (m0, z1, z2, z3):
        out[:EDGE] = msg_grad[:, :HALF]
    m1[...] = msg_grad[:, HALF:]
    for part in range(2):
        term[part * HALF : (part + 1) * HALF] = lax.dot_general(
            aggregated[part], act_grad, (((0,), (0,)), ((), ())), preferred_element_type=F32
        )
    zl = lax.axis_index("col") & 3
    for k, (out, base) in enumerate(((weight_own, 0), (z1, EDGE), (z2, EDGE), (z3, EDGE))):
        rows = pl.ds(pl.multiple_of(((zl + k) & 3) * 64, 64), 64)
        for side in range(2):
            first = base + side * 64
            out[first : first + 64] = term[rows, side * HALF : (side + 1) * HALF].astype(out.dtype)


def dense_call(sums, weight, grad_out):
    return small_call(
        dense_kernel,
        "dense",
        [(grad_out.shape, BF16), ((HALF, HALF), F32), ((EDGE, HALF), BF16)]
        + [((EDGE + HALF, HALF), BF16)] * 3
        + [((EDGE, HALF), BF16)],
        (*sums, weight, grad_out),
        [pltpu.VMEM((EDGE, EDGE), F32)],
        6 * 256**3,
    )


def pack_kernel(m0, z1, z2, z3, weight_own, group):
    term = weight_own[...]
    for piece in (z1, z2, z3):
        term = term + piece[EDGE:].astype(F32)
    for j, piece in enumerate((m0, z1, z2, z3)):
        group[j * EDGE : (j + 1) * EDGE] = piece[:EDGE]
    group[GROUP:] = term.astype(BF16)


def pack_call(m0, received, weight_own):
    return small_call(
        pack_kernel,
        "pack_messages",
        [((GROUP + WEIGHT_ROWS, HALF), BF16)],
        (m0, *received, weight_own),
    )[0]


def add_y_kernel(q0, q1, q2, q3, kept, given, buf):
    quads = (q0, q1, q2, q3)
    total = quads[0][...].astype(F32)
    for quad in quads[1:]:
        total = total + quad[...].astype(F32)
    kept[...] = total[:EDGE]
    given[:EDGE] = total[EDGE : 2 * EDGE].astype(BF16)
    if given.shape[0] > EDGE:
        for k, quad in enumerate(quads):
            buf[k] = quad[2 * EDGE :].astype(F32)
        y = (lax.axis_index("row") >> 1) & 3
        term = buf[y]
        for place in range(1, 4):
            term = term + buf[(y - place) & 3]
        given[EDGE:] = term.astype(BF16)


def add_y_call(quads):
    rows = quads[0].shape[0]
    return small_call(
        add_y_kernel,
        "add_over_y",
        [((EDGE, HALF), F32), ((rows - EDGE, HALF), BF16)],
        quads,
        [pltpu.VMEM((4, WEIGHT_ROWS, HALF), F32)],
    )


def spread_kernel(scale, a0, a1, a2, a3, out):
    col = lax.axis_index("col")
    for k, piece in enumerate((a0, a1, a2, a3)):
        row = pl.multiple_of(((col - k) & 3) * 64, 64)
        for side in range(2):
            out[pl.ds(row, 64), side * HALF : (side + 1) * HALF] = piece[side * 64 : side * 64 + 64] * scale


def add_all(pieces):
    total = pieces[0].astype(F32)
    for piece in pieces[1:]:
        total = total + piece.astype(F32)
    return total


def local(features, adj_tiles, tile_rows, tile_cols, tile_count, weight, grad_out):
    tiles = adj_tiles[0, 0]
    row_ids, col_ids, count = tile_rows[0, 0], tile_cols[0, 0], tile_count[0]
    node_total = EDGE * ROW_DEVICES * COL_DEVICES

    with jax.named_scope("gather_features"):
        other = row_permute(features, zh=1)
        pairs = [
            jnp.stack([value[:, h * HALF : (h + 1) * HALF] for value in (features, other)]) for h in range(2)
        ]
    for h in range(2):
        with jax.named_scope("gather_features"):
            near = jnp.concatenate([pairs[h]] + [row_permute(pairs[h], y=k) for k in (1, 2, 3)])
            if h == 1:
                near, before = lax.optimization_barrier((near, parts))
            far = row_permute(near, core=1)
            if h == 0:
                far, pairs[1] = lax.optimization_barrier((far, pairs[1]))
        parts = tile_call(
            forward_kernel, "forward_tiles", count, row_ids, col_ids, [near, far], tiles, [(4, EDGE, HALF)] * 4
        )
    sums = []
    for parts in (before, parts):
        with jax.named_scope("reduce_aggregate"):
            parts = [parts[0]] + [col_permute(parts[k], x=k) for k in (1, 2, 3)]
            part_sums = [add_all([part[j] for part in parts]) for j in range(4)]
            sums += [part_sums[0]] + [col_permute(part_sums[k].astype(BF16), zl=k) for k in (1, 2, 3)]

    activation, weight_own, m0, z1, z2, z3, m1 = dense_call(sums, weight, grad_out)

    with jax.named_scope("gather_messages"):
        arrived = [col_permute(z, zl=k) for k, z in ((1, z1), (2, z2), (3, z3))]
        group = pack_call(m0, arrived, weight_own)
        first = [group] + [col_permute(group, x=k) for k in (1, 2, 3)]
        group = jnp.concatenate([m1] + [col_permute(m1, zl=k) for k in (1, 2, 3)])
        first, group = lax.optimization_barrier((first, group))
        second = [group] + [col_permute(group, x=k) for k in (1, 2, 3)]

    def products(h, group):
        return tile_call(
            functools.partial(backward_kernel, h == 0),
            "backward_tiles",
            count,
            col_ids,
            row_ids,
            group,
            tiles,
            [(4, 2 * EDGE + (WEIGHT_ROWS if h == 0 else 0), HALF)] * 2,
            h == 0,
        )

    def add_core(own, sent):
        both = add_all([own, row_permute(sent, core=1)]).astype(BF16)
        return [both[0]] + [row_permute(both[k], y=k) for k in (1, 2, 3)]

    own, sent = products(0, first)
    beside = [1, 3]
    own, sent, arrived = lax.optimization_barrier((own, sent, [second[k] for k in beside]))
    for k, value in zip(beside, arrived):
        second[k] = value
    with jax.named_scope("reduce_features"):
        quads = add_core(own, sent)
    own, sent = products(1, second)
    own, sent, quads = lax.optimization_barrier((own, sent, quads))
    with jax.named_scope("reduce_features"):
        kept0, given0 = add_y_call(quads)
        last0 = row_permute(given0, zh=1)
        kept1, given1 = add_y_call(add_core(own, sent))
        last1 = row_permute(given1, zh=1)
        halves = [kept0 + last0[:EDGE].astype(F32), kept1 + last1.astype(F32)]
    with jax.named_scope("gather_weight"):
        mine = given0[EDGE:].astype(F32) + last0[EDGE:].astype(F32)
        mine = [mine] + [col_permute(mine, zl=k) for k in (1, 2, 3)]
    x_grad = jnp.concatenate(halves, axis=1).astype(BF16)
    weight_grad = small_call(
        functools.partial(spread_kernel, 1.0 / math.sqrt(node_total)), "spread_weight", [((EDGE, EDGE), F32)], mine
    )[0]

    return (activation, weight_grad, x_grad)


def solution(mesh):
    return jax.shard_map(
        local,
        mesh=mesh,
        in_specs=(
            P(("col", "row"), None),
            P("row", "col", None, None, None),
            P("row", "col", None),
            P("row", "col", None),
            P("row", "col"),
            P(),
            P(("row", "col"), None),
        ),
        out_specs=(P(("row", "col"), None), P(), P(("col", "row"), None)),
        check_vma=False,
    )
```
